256 devices in a mesh: blk: 16 (over y, x_lo, core), rep: 16 (over z, x_hi).
Axes of the slice: x: 4 (x_hi: 2, x_lo: 2; x = x_hi * 2 + x_lo), y: 4, z: 8, core: 2. Of those that a mesh axis runs over, the one named last changes fastest.
Arguments:
- features: bfloat16 [65536, 128], P(('blk', 'rep')), may hold values from -6 to 6
- edge_rows: int32 [16, 16, 32, 256], P('blk', None, 'rep'), may hold values from 0 to 4095
- edge_cols: int32 [16, 16, 32, 256], P('blk', None, 'rep'), may hold values from 0 to 127
- weight: bfloat16 [128, 256], replicated, may hold values from -0.5 to 0.5
- bias: float32 [256], replicated, may hold values from -3 to 3
- upstream: bfloat16 [65536, 256], P('blk'), may hold values from -6 to 6
- train_mask: int32 [65536], P('blk'), may hold values 0 or 1
Outputs:
- activations: bfloat16 [65536, 256], P(('blk', 'rep'))
- grad_features: bfloat16 [65536, 128], P(('blk', 'rep'))
- grad_weight: float32 [128, 256], replicated
- grad_bias: float32 [256], replicated
The draws below stay inside these ranges and needn't reach their ends.
Inputs may be any that keep to these rules, and one draw needn't show every extreme that they name: `edge_rows`: target indices within a panel. `edge_cols`: source indices within a column block.
All inputs are finite; a program needn't handle non-finite values. No bound on the sum of `train_mask` on one device may be relied on, other than what follows from the above.
Results may differ from the reference program's by a relative error of at most 0.018.
Values may be sent and summed in bfloat16 or wider, within the bound.
No kernel may reach another device: no remote copies, remote signals or barrier semaphores. Data moves between devices by JAX's collectives and lax.ppermute only.
A program may use at most 64 MiB of HBM per device.

```python
import jax
import jax.numpy as jnp
from jax import lax

D_IN = 128
HID = 256
CB = 128
PIECE = 256
PANEL = 4096
NODES = 65536
BLOCKS = 32
EDGES = 256
N_BLK = 16
N_REP = 16


def touch_ends(drawn, rng, least, high):
    spot = [jax.random.randint(jax.random.fold_in(rng, axis), (), 0, length) for axis, length in enumerate(drawn.shape)]
    widest = drawn.shape.index(max(drawn.shape))
    neighbour = spot[:widest] + [(spot[widest] + 1) % drawn.shape[widest]] + spot[widest + 1:]
    return drawn.at[tuple(spot)].set(least).at[tuple(neighbour)].set(high)


def level_of(rng, dims, pieces, smallest, high):
    gain = 1.0
    for dim, shards_of in pieces:
        draws = jax.random.uniform(jax.random.fold_in(jax.random.fold_in(rng, 6), dim), (shards_of,), jnp.float32, smallest / len(pieces), high / len(pieces))
        gain = gain * jnp.repeat(jnp.exp(draws), dims[dim] // shards_of).reshape((-1,) + (1,) * (len(dims) - 1 - dim))
    return gain


def noise(rng, shape, width, limit, pieces=(), held_as=jnp.bfloat16):
    drawn = jax.random.normal(rng, shape, jnp.float32) * width
    if len(pieces) > 0:
        drawn = level_of(rng, shape, pieces, -0.22, 0.18) * drawn
    return jnp.clip(drawn, min=-limit, max=limit).astype(held_as)


def setup_inputs(seed: int = 0) -> dict:
    arg_keys = jax.random.split(jax.random.key(seed), 8)
    features = noise(arg_keys[0], (NODES, D_IN), 1.0, 6.0, ((0, 256),))
    edge_rows = touch_ends(jax.random.randint(arg_keys[1], (N_BLK, N_BLK, BLOCKS, EDGES), 0, PANEL), jax.random.fold_in(arg_keys[1], 1), 0, PANEL - 1).astype(jnp.int32)
    edge_cols = touch_ends(jax.random.randint(arg_keys[2], (N_BLK, N_BLK, BLOCKS, EDGES), 0, CB), jax.random.fold_in(arg_keys[2], 1), 0, CB - 1).astype(jnp.int32)
    weight = noise(arg_keys[3], (D_IN, HID), D_IN ** -0.5, 0.5)
    bias = noise(arg_keys[4], (HID,), 0.5, 3.0, (), jnp.float32)
    upstream = noise(arg_keys[5], (NODES, HID), 1.0, 6.0, ((0, 16),))
    train_mask = touch_ends((jax.random.randint(arg_keys[6], (NODES,), 0, 4) < 1).astype(jnp.int32), jax.random.fold_in(arg_keys[6], 1), 0, 1)
    return dict(features=features, edge_rows=edge_rows, edge_cols=edge_cols, weight=weight, bias=bias, upstream=upstream, train_mask=train_mask)


def reference(features, edge_rows, edge_cols, weight, bias, upstream, train_mask):
    npanel = PIECE * N_REP
    nodes = npanel * N_BLK
    group_size = PIECE // CB
    col_base = (jnp.arange(N_BLK, dtype=jnp.int32)[:, None, None] * npanel
                + jnp.arange(npanel // CB, dtype=jnp.int32)[None, :, None] * CB)
    group_of = (jnp.arange(npanel // CB, dtype=jnp.int32) // group_size)[None, :, None]
    feats = features.astype(jnp.float32)

    def panel_sum(panel):
        targets = edge_rows[panel]
        columns = edge_cols[panel]
        sources = (col_base + columns).reshape(-1)
        segment = (group_of * npanel + targets).reshape(-1)
        values = feats[sources]
        parts = jax.ops.segment_sum(values, segment, num_segments=N_REP * npanel)
        parts = parts.reshape(N_REP, npanel, D_IN)
        parts = lax.optimization_barrier(parts.astype(jnp.bfloat16)).astype(jnp.float32)
        counts = jax.ops.segment_sum(jnp.ones((targets.size,), jnp.float32), targets.reshape(-1), num_segments=npanel)
        return jnp.sum(parts, axis=0), counts

    gathered, counts = lax.map(panel_sum, jnp.arange(N_BLK, dtype=jnp.int32))
    gathered = gathered.reshape(nodes, D_IN)
    degree = 1.0 + counts.reshape(nodes)
    mixed_in = ((feats + gathered) / degree[:, None]).astype(jnp.bfloat16)
    pre_act = jnp.dot(mixed_in, weight, preferred_element_type=jnp.float32) + bias
    gate_value = jax.nn.sigmoid(pre_act)
    activations = (pre_act * gate_value).astype(jnp.bfloat16)
    slope = gate_value * (1.0 + pre_act * (1.0 - gate_value))
    grad_pre = (upstream.astype(jnp.float32) * train_mask.astype(jnp.float32)[:, None] * slope).astype(jnp.bfloat16)
    grad_weight = lax.dot_general(mixed_in, grad_pre, (((0,), (0,)), ((), ())), preferred_element_type=jnp.float32)
    grad_bias = jnp.sum(grad_pre.astype(jnp.float32), axis=0)
    scaled_back = (jnp.dot(grad_pre, weight.T, preferred_element_type=jnp.float32) / degree[:, None]).astype(jnp.bfloat16)

    def scatter_back(running, panel):
        targets = edge_rows[panel]
        columns = edge_cols[panel]
        sources = (col_base + columns).reshape(-1)
        own_back = lax.dynamic_slice_in_dim(scaled_back, panel * npanel, npanel, 0)
        values = own_back[targets.reshape(-1)].astype(jnp.float32)
        return running + jax.ops.segment_sum(values, sources, num_segments=nodes), None

    received, _ = lax.scan(scatter_back, jnp.zeros((nodes, D_IN), jnp.float32), jnp.arange(N_BLK, dtype=jnp.int32))
    grad_features = (scaled_back.astype(jnp.float32) + received).astype(jnp.bfloat16)
    return activations, grad_features, grad_weight, grad_bias
```

```python
import functools

import jax
import jax.numpy as jnp
from jax import lax
from jax.experimental import pallas as pl
from jax.experimental.pallas import tpu as pltpu
from jax.sharding import PartitionSpec as P

CB = 128
LANES = 128
BF = jnp.bfloat16
F32 = jnp.float32
TN = (((0,), (0,)), ((), ()))
NT = (((1,), (1,)), ((), ()))
ACCS = 4
UNROLL = 16

VMEM = pl.BlockSpec(memory_space=pltpu.VMEM)
SMEM = pl.BlockSpec(memory_space=pltpu.SMEM)


def exchange(parts, axis):
    return lax.all_to_all(parts, axis, split_axis=0, concat_axis=0, tiled=True)


def from_everyone(value, axis):
    return exchange(jnp.broadcast_to(value, (lax.axis_size(axis), *value.shape)), axis)


def one_hot(index, count):
    hits = lax.broadcasted_iota(jnp.int32, (count, index.shape[-1]), 0) == index
    return hits.astype(F32).astype(BF)


def count_kernel(rows_ref, out_ref):
    rows = rows_ref[...]
    total = jnp.zeros(out_ref.shape, F32)
    for k in range(rows.shape[0]):
        index = rows[k : k + 1, :]
        high = one_hot(jnp.right_shift(index, 7), out_ref.shape[0])
        low = one_hot(jnp.bitwise_and(index, LANES - 1), LANES)
        total += lax.dot_general(high, low, NT, preferred_element_type=F32)
    out_ref[...] = total


def gather_sum_kernel(rows_ref, sources_ref, table_ref, counts_ref, out_ref, wide_ref, *totals):
    pieces = out_ref.shape[0]
    piece_rows = wide_ref.shape[0] // pieces
    edges = rows_ref.shape[0] * rows_ref.shape[1]
    wide_ref[...] = table_ref[...].astype(F32)
    for total in totals:
        total[...] = jnp.zeros_like(total)

    @pl.loop(0, rows_ref.shape[0])
    def _(i):
        for u in range(0, UNROLL, ACCS):
            rows = [rows_ref[i, u + j] for j in range(ACCS)]
            values = [wide_ref[pl.ds(sources_ref[i, u + j], 1), :] for j in range(ACCS)]
            olds = [totals[j][pl.ds(rows[j], 1), :] for j in range(ACCS)]
            for j in range(ACCS):
                totals[j][pl.ds(rows[j], 1), :] = olds[j] + values[j]

    @pl.loop(0, pieces)
    def _(p):
        span = pl.ds(p * piece_rows, piece_rows)
        part = totals[0][span, :]
        for total in totals[1:]:
            part += total[span, :]
        out_ref[p, :piece_rows, :] = part.astype(BF)
        groups = piece_rows // LANES
        count = counts_ref[pl.ds(p * groups, groups), :]
        high = jnp.floor(count * (1.0 / 128.0))
        low = count - high * 128.0
        rest = jnp.zeros((8 - 2 * groups, LANES), F32)
        out_ref[p, piece_rows:, :] = jnp.concatenate([high, low, rest], 0).astype(BF)


def spread_kernel(rows_ref, cols_ref, table_ref, out_ref, wide_ref, picked_ref):
    wide_ref[...] = table_ref[...].astype(F32)
    slots = cols_ref.shape[1]
    steps = slots // UNROLL

    @pl.loop(0, cols_ref.shape[0])
    def _(k):
        @pl.loop(0, steps)
        def _(i):
            for u in range(UNROLL):
                picked_ref[pl.ds(i * UNROLL + u, 1), :] = wide_ref[
                    pl.ds(rows_ref[k * steps + i, u], 1), :
                ]

        hits = one_hot(cols_ref[pl.ds(k, 1), :], CB)
        terms = jnp.dot(hits, picked_ref[...].astype(BF), preferred_element_type=F32)
        out_ref[pl.ds(pl.multiple_of(k * CB, CB), CB), :] = terms.astype(BF)


def as_column(row):
    size = row.shape[1]
    diagonal = lax.broadcasted_iota(jnp.int32, (size, size), 0) == lax.broadcasted_iota(
        jnp.int32, (size, size), 1
    )
    return jnp.sum(jnp.where(diagonal, row, 0.0), axis=1, keepdims=True)


def dense_kernel(
    place_ref, parts_ref, feats_ref, upstream_ref, mask_ref, weight_ref, bias_ref,
    act_ref, back_ref, wpart_ref, bpart_ref,
):
    piece_rows, width = feats_ref.shape
    total = parts_ref[0].astype(F32)
    for p in range(1, parts_ref.shape[0]):
        total += parts_ref[p].astype(F32)
    groups = piece_rows // LANES
    counts = total[piece_rows : piece_rows + groups] * 128.0 + total[
        piece_rows + groups : piece_rows + 2 * groups
    ]
    degree = 1.0 + jnp.concatenate([as_column(counts[g : g + 1]) for g in range(groups)], 0)
    mask = jnp.concatenate([as_column(mask_ref[g : g + 1].astype(F32)) for g in range(groups)], 0)
    mixed = ((feats_ref[...].astype(F32) + total[:piece_rows]) / degree).astype(BF)
    weight = weight_ref[...]
    pre = jnp.dot(mixed, weight, preferred_element_type=F32) + bias_ref[...]
    gate = 1.0 / (1.0 + jnp.exp(-pre))
    act_ref[...] = (pre * gate).astype(BF)
    slope = gate * (1.0 + pre * (1.0 - gate))
    grad = (upstream_ref[...].astype(F32) * mask * slope).astype(BF)
    back = lax.dot_general(grad, weight, NT, preferred_element_type=F32) / degree
    back_ref[...] = back.astype(BF)
    wpart_ref[...] = lax.dot_general(mixed, grad, TN, preferred_element_type=F32)
    bpart_ref[...] = jnp.sum(grad.astype(F32), axis=0, keepdims=True)


def close_kernel(terms_ref, back_ref, out_ref):
    total = back_ref[...].astype(F32)
    for p in range(terms_ref.shape[0]):
        total += terms_ref[p].astype(F32)
    out_ref[...] = total.astype(BF)


def on_device(features, edge_rows, edge_cols, weight, bias, upstream, train_mask):
    piece_rows, width = features.shape
    hidden = weight.shape[1]
    slots = edge_rows.shape[-1]
    panel_rows = upstream.shape[0]
    n_blk, n_rep = lax.axis_size("blk"), lax.axis_size("rep")
    place = lax.axis_index("rep")
    rows = edge_rows.reshape(-1, slots)
    cols = edge_cols.reshape(-1, slots)
    blocks = rows.shape[0]
    edges = blocks * slots

    table = from_everyone(features, "blk").reshape(n_blk * piece_rows, width)
    counts = pl.pallas_call(
        count_kernel,
        in_specs=[VMEM],
        out_specs=VMEM,
        out_shape=jax.ShapeDtypeStruct((panel_rows // LANES, LANES), F32),
        name="count",
    )(rows)
    sources = cols + (jnp.arange(blocks, dtype=jnp.int32) * CB)[:, None]
    row_list = rows.reshape(-1, UNROLL)
    source_list = sources.reshape(-1, UNROLL)

    sends = pl.pallas_call(
        gather_sum_kernel,
        in_specs=[SMEM, SMEM, VMEM, VMEM],
        out_specs=VMEM,
        out_shape=jax.ShapeDtypeStruct((n_rep, piece_rows + 8, width), BF),
        scratch_shapes=[pltpu.VMEM((panel_rows, width), F32)] * (ACCS + 1),
        name="gather_sum",
    )(row_list, source_list, table, counts)
    parts = exchange(sends, "rep")

    activations, back, weight_part, bias_part = pl.pallas_call(
        dense_kernel,
        grid_spec=pltpu.PrefetchScalarGridSpec(
            num_scalar_prefetch=1,
            grid=(1,),
            in_specs=[
                pl.BlockSpec(parts.shape, lambda i, s: (0, 0, 0)),
                pl.BlockSpec(features.shape, lambda i, s: (0, 0)),
                pl.BlockSpec((piece_rows, hidden), lambda i, s: (s[0], 0)),
                pl.BlockSpec((None, piece_rows // LANES, LANES), lambda i, s: (s[0], 0, 0)),
                pl.BlockSpec(weight.shape, lambda i, s: (0, 0)),
                pl.BlockSpec((1, hidden), lambda i, s: (0, 0)),
            ],
            out_specs=[
                pl.BlockSpec((piece_rows, hidden), lambda i, s: (0, 0)),
                pl.BlockSpec((piece_rows, width), lambda i, s: (0, 0)),
                pl.BlockSpec((width, hidden), lambda i, s: (0, 0)),
                pl.BlockSpec((1, hidden), lambda i, s: (0, 0)),
            ],
        ),
        out_shape=[
            jax.ShapeDtypeStruct((piece_rows, hidden), BF),
            jax.ShapeDtypeStruct((piece_rows, width), BF),
            jax.ShapeDtypeStruct((width, hidden), F32),
            jax.ShapeDtypeStruct((1, hidden), F32),
        ],
        name="dense",
    )(
        place.astype(jnp.int32).reshape(1),
        parts,
        features,
        upstream,
        train_mask.reshape(n_rep, piece_rows // LANES, LANES),
        weight,
        bias.reshape(1, hidden),
    )

    back_panel = from_everyone(back, "rep").reshape(panel_rows, width)

    share = width // n_blk
    slim = hidden // n_blk
    both = jnp.concatenate(
        [
            weight_part.reshape(n_blk, share * hidden // LANES, LANES),
            jnp.pad(bias_part.reshape(n_blk, 1, slim), ((0, 0), (0, 7), (0, LANES - slim))),
        ],
        axis=1,
    )
    mine = jnp.sum(exchange(both, "blk"), axis=0)
    mine = jnp.sum(from_everyone(mine, "rep"), axis=0)
    whole = from_everyone(mine, "blk")
    grad_weight = whole[:, : share * hidden // LANES].reshape(width, hidden)
    grad_bias = whole[:, share * hidden // LANES, :slim].reshape(hidden)

    terms = pl.pallas_call(
        spread_kernel,
        in_specs=[SMEM, VMEM, VMEM],
        out_specs=VMEM,
        out_shape=jax.ShapeDtypeStruct((n_blk * piece_rows, width), BF),
        scratch_shapes=[pltpu.VMEM((panel_rows, width), F32), pltpu.VMEM((slots, width), F32)],
        name="spread",
    )(row_list, cols, back_panel)
    received = exchange(terms.reshape(n_blk, piece_rows, width), "blk")
    grad_features = pl.pallas_call(
        close_kernel,
        in_specs=[VMEM, VMEM],
        out_specs=VMEM,
        out_shape=jax.ShapeDtypeStruct((piece_rows, width), BF),
        name="close",
    )(received, back)
    return (activations, grad_features, grad_weight, grad_bias)


def solution(mesh):
    return jax.shard_map(
        on_device,
        mesh=mesh,
        in_specs=(
            P(("blk", "rep"), None),
            P("blk", None, "rep", None),
            P("blk", None, "rep", None),
            P(),
            P(),
            P("blk", None),
            P("blk"),
        ),
        out_specs=(P(("blk", "rep"), None), P(("blk", "rep"), None), P(), P()),
        check_vma=False,
    )
```

```python
import jax
import jax.numpy as jnp
from jax import lax
from jax.experimental import pallas as pl
from jax.experimental.pallas import tpu as pltpu
from jax.sharding import PartitionSpec as P


CB = 128
LANES = 128
BF = jnp.bfloat16
F32 = jnp.float32
TN = (((0,), (0,)), ((), ()))
NT = (((1,), (1,)), ((), ()))
TOTALS = 8
CHUNK = 1024

VMEM = pl.BlockSpec(memory_space=pltpu.VMEM)
ANY = pl.BlockSpec(memory_space=pl.ANY)


def cost(us):
    return pl.CostEstimate(flops=0, transcendentals=0, bytes_accessed=int(us * 3.0e6))


def exchange(parts, axis):
    return lax.all_to_all(parts, axis, split_axis=0, concat_axis=0, tiled=True)


def from_everyone(value, axis):
    return exchange(jnp.broadcast_to(value, (lax.axis_size(axis), *value.shape)), axis)


def one_hot(index, count):
    hits = lax.broadcasted_iota(jnp.int32, (count, index.shape[-1]), 0) == index
    return hits.astype(F32).astype(BF)


def count_kernel(rows_ref, out_ref):
    rows = rows_ref[...]
    total = jnp.zeros(out_ref.shape, F32)
    for k in range(rows.shape[0]):
        index = rows[k : k + 1, :]
        high = one_hot(jnp.right_shift(index, 7), out_ref.shape[0])
        low = one_hot(jnp.bitwise_and(index, LANES - 1), LANES)
        total += lax.dot_general(high, low, NT, preferred_element_type=F32)
    out_ref[...] = total


def gather_sum_kernel(
    rows_ref, cols_ref, table_ref, counts_ref, out_ref, list0, list1, sems, values0, values1, *totals
):
    lists, values = (list0, list1), (values0, values1)
    pieces = out_ref.shape[0]
    piece_rows = totals[0].shape[0] // pieces
    blocks, slots = cols_ref.shape
    held = CHUNK // slots
    steps = blocks // held // 2

    def fetch(step, side):
        return pltpu.make_async_copy(rows_ref.at[pl.ds(step * CHUNK, CHUNK)], lists[side], sems.at[side])

    def pick(k, side):
        hits = one_hot(cols_ref[pl.ds(k, 1), :], CB)
        block = table_ref[pl.ds(pl.multiple_of(k * CB, CB), CB), :]
        values[side][...] = lax.dot_general(hits, block, TN, preferred_element_type=F32)

    for side in range(2):
        fetch(side, side).start()
    for total in totals:
        total[...] = jnp.zeros_like(total)
    pick(0, 0)

    @pl.loop(0, steps)
    def _(i):
        for side in range(2):
            fetch(2 * i + side, side).wait()
            for s in range(held):
                pick(jnp.minimum((2 * i + side) * held + s + 1, blocks - 1), (s + 1) % 2)
                for u in range(0, slots, TOTALS):
                    rows = [lists[side][s * slots + u + j] for j in range(TOTALS)]
                    olds = [totals[j][pl.ds(rows[j], 1), :] for j in range(TOTALS)]
                    for j in range(TOTALS):
                        new = olds[j] + values[s % 2][u + j : u + j + 1, :]
                        totals[j][pl.ds(rows[j], 1), :] = new

            @pl.when(i < steps - 1)
            def _():
                fetch(2 * i + side + 2, side).start()

    @pl.loop(0, pieces)
    def _(p):
        span = pl.ds(p * piece_rows, piece_rows)
        part = totals[0][span, :]
        for total in totals[1:]:
            part += total[span, :]
        out_ref[p, :piece_rows, :] = part.astype(BF)
        groups = piece_rows // LANES
        count = counts_ref[pl.ds(p * groups, groups), :]
        high = jnp.floor(count * (1.0 / 128.0))
        low = count - high * 128.0
        rest = jnp.zeros((8 - 2 * groups, LANES), F32)
        out_ref[p, piece_rows:, :] = jnp.concatenate([high, low, rest], 0).astype(BF)


def spread_kernel(rows_ref, cols_ref, table_ref, out_ref, list0, list1, sems, wide_ref, picked0, picked1):
    lists, picked = (list0, list1), (picked0, picked1)
    pieces = table_ref.shape[0]
    piece_rows = wide_ref.shape[0] // pieces
    blocks, slots = cols_ref.shape
    held = CHUNK // slots
    steps = blocks // held // 2

    def fetch(step, side):
        return pltpu.make_async_copy(rows_ref.at[pl.ds(step * CHUNK, CHUNK)], lists[side], sems.at[side])

    for side in range(2):
        fetch(side, side).start()
    for p in range(pieces):
        wide_ref[p * piece_rows : (p + 1) * piece_rows, :] = table_ref[p, :piece_rows, :].astype(F32)

    @pl.loop(0, steps)
    def _(i):
        for side in range(2):
            fetch(2 * i + side, side).wait()
            for s in range(held):
                k = (2 * i + side) * held + s
                for u in range(slots):
                    row = wide_ref[pl.ds(lists[side][s * slots + u], 1), :]
                    picked[s % 2][u : u + 1, :] = row
                hits = one_hot(cols_ref[pl.ds(k, 1), :], CB)
                terms = jnp.dot(hits, picked[s % 2][...].astype(BF), preferred_element_type=F32)
                out_ref[pl.ds(pl.multiple_of(k * CB, CB), CB), :] = terms.astype(BF)

            @pl.when(i < steps - 1)
            def _():
                fetch(2 * i + side + 2, side).start()


def as_column(row):
    size = row.shape[1]
    diagonal = lax.broadcasted_iota(jnp.int32, (size, size), 0) == lax.broadcasted_iota(
        jnp.int32, (size, size), 1
    )
    return jnp.sum(jnp.where(diagonal, row, 0.0), axis=1, keepdims=True)


def dense_kernel(
    place_ref, parts_ref, feats_ref, upstream_ref, mask_ref, weight_ref, bias_ref,
    act_ref, back_ref, sends_ref,
):
    piece_rows, width = feats_ref.shape
    total = parts_ref[0].astype(F32)
    for p in range(1, parts_ref.shape[0]):
        total += parts_ref[p].astype(F32)
    groups = piece_rows // LANES
    counts = total[piece_rows : piece_rows + groups] * 128.0 + total[
        piece_rows + groups : piece_rows + 2 * groups
    ]
    degree = 1.0 + jnp.concatenate([as_column(counts[g : g + 1]) for g in range(groups)], 0)
    mask = jnp.concatenate([as_column(mask_ref[g : g + 1].astype(F32)) for g in range(groups)], 0)
    mixed = ((feats_ref[...].astype(F32) + total[:piece_rows]) / degree).astype(BF)
    weight = weight_ref[...]
    pre = jnp.dot(mixed, weight, preferred_element_type=F32) + bias_ref[...]
    gate = 1.0 / (1.0 + jnp.exp(-pre))
    act_ref[...] = (pre * gate).astype(BF)
    slope = gate * (1.0 + pre * (1.0 - gate))
    grad = (upstream_ref[...].astype(F32) * mask * slope).astype(BF)
    back = lax.dot_general(grad, weight, NT, preferred_element_type=F32) / degree
    back = back.astype(BF)
    back_ref[...] = back
    weight_part = lax.dot_general(mixed, grad, TN, preferred_element_type=F32).astype(BF)
    bias_part = jnp.sum(grad.astype(F32), axis=0, keepdims=True)
    spans = range(0, bias_part.shape[1], LANES)
    rest = jnp.zeros((8 - len(spans), LANES), F32)
    bias_part = jnp.concatenate([bias_part[:, c : c + LANES] for c in spans] + [rest], 0).astype(BF)
    share = width // sends_ref.shape[0]
    for p in range(sends_ref.shape[0]):
        pieces = [weight_part[p * share : (p + 1) * share, c : c + LANES] for c in spans]
        sends_ref[p] = jnp.concatenate([back, *pieces, bias_part], 0)


def close_kernel(terms_ref, back_ref, out_ref):
    total = back_ref[...].astype(F32)
    for p in range(terms_ref.shape[0]):
        total += terms_ref[p].astype(F32)
    out_ref[...] = total.astype(BF)


def layer(features, edge_rows, edge_cols, weight, bias, upstream, train_mask):
    piece_rows, width = features.shape
    hidden = weight.shape[1]
    slots = edge_rows.shape[-1]
    panel_rows = upstream.shape[0]
    n_blk, n_rep = lax.axis_size("blk"), lax.axis_size("rep")
    place = lax.axis_index("rep")
    rows = edge_rows.reshape(-1, slots)
    cols = edge_cols.reshape(-1, slots)

    table = from_everyone(features, "blk").reshape(n_blk * piece_rows, width)
    counts = pl.pallas_call(
        count_kernel,
        in_specs=[VMEM],
        out_specs=VMEM,
        out_shape=jax.ShapeDtypeStruct((panel_rows // LANES, LANES), F32),
        cost_estimate=cost(2),
        name="count",
    )(rows)
    row_list = rows.reshape(-1)
    chunks = [pltpu.SMEM((CHUNK,), jnp.int32)] * 2 + [pltpu.SemaphoreType.DMA((2,))]

    sends = pl.pallas_call(
        gather_sum_kernel,
        in_specs=[ANY, VMEM, VMEM, VMEM],
        out_specs=VMEM,
        out_shape=jax.ShapeDtypeStruct((n_rep, piece_rows + 8, width), BF),
        scratch_shapes=chunks
        + [pltpu.VMEM((slots, width), F32)] * 2
        + [pltpu.VMEM((panel_rows, width), F32)] * TOTALS,
        cost_estimate=cost(14),
        name="gather_sum",
    )(row_list, cols, table, counts)
    parts = exchange(sends, "rep")

    share = width // n_rep
    spans = hidden // LANES
    extra = share * spans + 8
    activations, back, sends = pl.pallas_call(
        dense_kernel,
        grid_spec=pltpu.PrefetchScalarGridSpec(
            num_scalar_prefetch=1,
            grid=(1,),
            in_specs=[
                pl.BlockSpec(parts.shape, lambda i, s: (0, 0, 0)),
                pl.BlockSpec(features.shape, lambda i, s: (0, 0)),
                pl.BlockSpec((piece_rows, hidden), lambda i, s: (s[0], 0)),
                pl.BlockSpec((None, piece_rows // LANES, LANES), lambda i, s: (s[0], 0, 0)),
                pl.BlockSpec(weight.shape, lambda i, s: (0, 0)),
                pl.BlockSpec((1, hidden), lambda i, s: (0, 0)),
            ],
            out_specs=[
                pl.BlockSpec((piece_rows, hidden), lambda i, s: (0, 0)),
                pl.BlockSpec((piece_rows, width), lambda i, s: (0, 0)),
                pl.BlockSpec((n_rep, piece_rows + extra, width), lambda i, s: (0, 0, 0)),
            ],
        ),
        out_shape=[
            jax.ShapeDtypeStruct((piece_rows, hidden), BF),
            jax.ShapeDtypeStruct((piece_rows, width), BF),
            jax.ShapeDtypeStruct((n_rep, piece_rows + extra, width), BF),
        ],
        cost_estimate=cost(3),
        name="dense",
    )(
        place.astype(jnp.int32).reshape(1),
        parts,
        features,
        upstream,
        train_mask.reshape(n_rep, piece_rows // LANES, LANES),
        weight,
        bias.reshape(1, hidden),
    )

    panel = exchange(sends, "rep")

    mine = jnp.sum(panel[:, piece_rows:].astype(F32), axis=0)
    arrived = from_everyone(mine, "blk")
    terms = pl.pallas_call(
        spread_kernel,
        in_specs=[ANY, VMEM, VMEM],
        out_specs=VMEM,
        out_shape=jax.ShapeDtypeStruct((n_blk * piece_rows, width), BF),
        scratch_shapes=chunks
        + [pltpu.VMEM((panel_rows, width), F32)]
        + [pltpu.VMEM((slots, width), F32)] * 2,
        cost_estimate=cost(14),
        name="spread",
    )(row_list, cols, panel)
    terms, arrived = lax.optimization_barrier((terms, arrived))
    received = exchange(terms.reshape(n_blk, piece_rows, width), "blk")
    mine = jnp.sum(arrived, axis=0)
    grad_bias = mine[share * spans : share * spans + spans].reshape(hidden)
    whole = mine[: share * spans][None]
    for bit in (8, 4, 1, 2):
        theirs = lax.ppermute(whole, "rep", [(i, i ^ bit) for i in range(n_rep)])
        upper = jnp.bitwise_and(place, bit) != 0
        whole = jnp.stack([jnp.where(upper, theirs, whole), jnp.where(upper, whole, theirs)], 0)
        whole = whole.reshape(-1, share * spans, LANES)
    whole = whole.reshape(2, 2, 2, 2, spans, share, LANES)
    whole = whole.transpose(3, 2, 0, 1, 5, 4, 6)
    grad_weight = whole.reshape(width, hidden)

    grad_features = pl.pallas_call(
        close_kernel,
        in_specs=[VMEM, VMEM],
        out_specs=VMEM,
        out_shape=jax.ShapeDtypeStruct((piece_rows, width), BF),
        cost_estimate=cost(1),
        name="close",
    )(received, back)
    return (activations, grad_features, grad_weight, grad_bias)


def solution(mesh):
    return jax.shard_map(
        layer,
        mesh=mesh,
        in_specs=(
            P(("blk", "rep"), None),
            P("blk", None, "rep", None),
            P("blk", None, "rep", None),
            P(),
            P(),
            P("blk", None),
            P("blk"),
        ),
        out_specs=(P(("blk", "rep"), None), P(("blk", "rep"), None), P(), P()),
        check_vma=False,
    )
```

```python
import functools

import jax
import jax.numpy as jnp
from jax import lax
from jax.experimental import pallas as pl
from jax.experimental.pallas import tpu as pltpu
from jax.sharding import PartitionSpec as P


CB = 128
LANES = 128
HALF = 64
BF = jnp.bfloat16
F32 = jnp.float32
TN = (((0,), (0,)), ((), ()))
NT = (((1,), (1,)), ((), ()))
TOTALS = 8
CHUNK = 1024

VMEM = pl.BlockSpec(memory_space=pltpu.VMEM)
ANY = pl.BlockSpec(memory_space=pl.ANY)
SMEM = pl.BlockSpec(memory_space=pltpu.SMEM)


def cost(us):
    return pl.CostEstimate(flops=0, transcendentals=0, bytes_accessed=int(us * 3.0e6))


def exchange(parts, axis, groups=None):
    return lax.all_to_all(
        parts, axis, split_axis=0, concat_axis=0, tiled=True, axis_index_groups=groups
    )


def swapped(value, axis, count, bits):
    return lax.ppermute(value, axis, [(i, i ^ bits) for i in range(count)])


def one_hot(index, count):
    hits = lax.broadcasted_iota(jnp.int32, (count, index.shape[-1]), 0) == index
    return hits.astype(F32).astype(BF)


def turned(value):
    return pltpu.roll(value, HALF, 1)


def left_lanes(rows):
    return lax.broadcasted_iota(jnp.int32, (rows, LANES), 1) < HALF


def unpacked(first, second):
    left = left_lanes(first.shape[0])
    top = jnp.where(left, first, turned(second))
    bottom = jnp.where(left, turned(first), second)
    return jnp.concatenate([top, bottom], 0)


def packed(rows):
    half = rows.shape[0] // 2
    left = left_lanes(half)
    top, bottom = rows[:half], rows[half:]
    return jnp.where(left, top, turned(bottom)), jnp.where(left, turned(top), bottom)


def count_kernel(rows_ref, out_ref):
    rows = rows_ref[...]
    total = jnp.zeros(out_ref.shape, F32)
    for k in range(rows.shape[0]):
        index = rows[k : k + 1, :]
        high = one_hot(jnp.right_shift(index, 7), out_ref.shape[0])
        low = one_hot(jnp.bitwise_and(index, LANES - 1), LANES)
        total += lax.dot_general(high, low, NT, preferred_element_type=F32)
    out_ref[...] = total


def gather_sum_kernel(closing, place_ref, rows_ref, cols_ref, table_ref, *refs):
    if closing:
        counts_ref, before_ref, out_ref, list0, list1, sems, values0, values1, held_ref, sem = refs[:10]
        totals = refs[10:]
        pltpu.make_async_copy(before_ref, held_ref, sem).start()
    else:
        out_ref, list0, list1, sems, values0, values1 = refs[:6]
        totals = refs[6:]
    lists, values = (list0, list1), (values0, values1)
    slots = cols_ref.shape[1]
    blocks = cols_ref.shape[0] // 2
    held = CHUNK // slots
    steps = blocks // held // 2
    core = jnp.bitwise_and(place_ref[1], 1)
    base = (1 - core if closing else core) * blocks

    def fetch(step, side):
        start = pl.multiple_of(base * slots + step * CHUNK, CHUNK)
        return pltpu.make_async_copy(rows_ref.at[pl.ds(start, CHUNK)], lists[side], sems.at[side])

    keep = left_lanes(CB).astype(F32).astype(BF)
    keeps = (keep, 1.0 - keep)

    def pick(k, side):
        hits = one_hot(cols_ref[pl.ds(base + k, 1), :], CB)
        block = table_ref[k >> 1] * keeps[side]
        values[side][...] = lax.dot_general(hits, block, TN, preferred_element_type=F32)

    for side in range(2):
        fetch(side, side).start()
    for total in totals:
        total[...] = jnp.zeros_like(total)
    pick(0, 0)

    @pl.loop(0, steps)
    def _(i):
        for side in range(2):
            fetch(2 * i + side, side).wait()
            for s in range(held):
                pick(jnp.minimum((2 * i + side) * held + s + 1, blocks - 1), (s + 1) % 2)
                for u in range(0, slots, TOTALS):
                    rows = [lists[side][s * slots + u + j] for j in range(TOTALS)]
                    olds = [totals[j][pl.ds(rows[j], 1), :] for j in range(TOTALS)]
                    for j in range(TOTALS):
                        new = olds[j] + values[s % 2][u + j : u + j + 1, :]
                        totals[j][pl.ds(rows[j], 1), :] = new

            @pl.when(i < steps - 1)
            def _():
                fetch(2 * i + side + 2, side).start()

    piece_rows = 2 * CB
    left = left_lanes(CB)
    if closing:
        pltpu.make_async_copy(before_ref, held_ref, sem).wait()

    @pl.loop(0, totals[0].shape[0] // piece_rows)
    def _(p):
        span = pl.ds(p * piece_rows, piece_rows)
        part = totals[0][span, :]
        for total in totals[1:]:
            part += total[span, :]
        if not closing:
            out_ref[span, :] = part
            return
        part += held_ref[span, :]
        part += turned(part)
        out_ref[p, :CB, :] = jnp.where(left, part[:CB], part[CB:]).astype(BF)
        groups = piece_rows // LANES
        count = counts_ref[pl.ds(p * groups, groups), :]
        high = jnp.floor(count * (1.0 / 128.0))
        low = count - high * 128.0
        rest = jnp.zeros((8 - 2 * groups, LANES), F32)
        out_ref[p, CB:, :] = jnp.concatenate([high, low, rest], 0).astype(BF)


def spread_kernel(
    own, place_ref, rows_ref, cols_ref, table_ref, out_ref, list0, list1, sems, wide_ref, picked0, picked1
):
    lists, picked = (list0, list1), (picked0, picked1)
    pieces, half = table_ref.shape[0], CB
    slots = cols_ref.shape[1]
    blocks = cols_ref.shape[0] // 2
    held = CHUNK // slots
    steps = blocks // held // 2
    core = jnp.bitwise_and(place_ref[1], 1)
    base = (core if own else 1 - core) * blocks

    def fetch(step, side):
        start = pl.multiple_of(base * slots + step * CHUNK, CHUNK)
        return pltpu.make_async_copy(rows_ref.at[pl.ds(start, CHUNK)], lists[side], sems.at[side])

    for side in range(2):
        fetch(side, side).start()
    for p in range(pieces):
        block = table_ref[p, :half, :].astype(F32)
        wide_ref[p * 2 * half : (p + 1) * 2 * half, :] = unpacked(block, block)
    left = left_lanes(CB)

    @pl.loop(0, steps)
    def _(i):
        for side in range(2):
            fetch(2 * i + side, side).wait()
            terms = [None, None]
            for s in range(held):
                k = (2 * i + side) * held + s
                for u in range(slots):
                    row = wide_ref[pl.ds(lists[side][s * slots + u], 1), :]
                    picked[s % 2][u : u + 1, :] = row
                hits = one_hot(cols_ref[pl.ds(base + k, 1), :], CB)
                terms[s % 2] = jnp.dot(hits, picked[s % 2][...].astype(BF), preferred_element_type=F32)
                if s % 2 == 1:
                    both = jnp.where(left, terms[0], terms[1]).astype(BF)
                    out_ref[k >> 1] = both

            @pl.when(i < steps - 1)
            def _():
                fetch(2 * i + side + 2, side).start()


def as_column(row):
    size = row.shape[1]
    diagonal = lax.broadcasted_iota(jnp.int32, (size, size), 0) == lax.broadcasted_iota(
        jnp.int32, (size, size), 1
    )
    return jnp.sum(jnp.where(diagonal, row, 0.0), axis=1, keepdims=True)


def dense_kernel(
    place_ref, parts_ref, feats_ref, upstream_ref, mask_ref, weight_ref, bias_ref,
    act_ref, back_ref, sends_ref,
):
    piece_rows, width = feats_ref.shape
    half = piece_rows // 2
    sums = [parts_ref[s].astype(F32) for s in range(2)]
    for p in range(2, parts_ref.shape[0]):
        sums[p % 2] += parts_ref[p].astype(F32)
    gathered = unpacked(sums[0][:half], sums[1][:half])
    groups = piece_rows // LANES
    numbers = sums[0][half:] + sums[1][half:]
    counts = numbers[:groups] * 128.0 + numbers[groups : 2 * groups]
    degree = 1.0 + jnp.concatenate([as_column(counts[g : g + 1]) for g in range(groups)], 0)
    mask = jnp.concatenate([as_column(mask_ref[g : g + 1].astype(F32)) for g in range(groups)], 0)
    mixed = ((feats_ref[...].astype(F32) + gathered) / degree).astype(BF)
    weight = weight_ref[...]
    pre = jnp.dot(mixed, weight, preferred_element_type=F32) + bias_ref[...]
    gate = 1.0 / (1.0 + jnp.exp(-pre))
    act_ref[...] = (pre * gate).astype(BF)
    slope = gate * (1.0 + pre * (1.0 - gate))
    grad = (upstream_ref[...].astype(F32) * mask * slope).astype(BF)
    back = lax.dot_general(grad, weight, NT, preferred_element_type=F32) / degree
    back = back.astype(BF)
    back_ref[...] = back
    sides = [side.astype(BF) for side in packed(back.astype(F32))]
    weight_part = lax.dot_general(mixed, grad, TN, preferred_element_type=F32).astype(BF)
    bias_part = jnp.sum(grad.astype(F32), axis=0, keepdims=True)
    spans = range(0, bias_part.shape[1], LANES)
    rest = jnp.zeros((8 - len(spans), LANES), F32)
    bias_part = jnp.concatenate([bias_part[:, c : c + LANES] for c in spans] + [rest], 0).astype(BF)
    share = width // sends_ref.shape[0]
    for p in range(sends_ref.shape[0]):
        pieces = [weight_part[p * share : (p + 1) * share, c : c + LANES] for c in spans]
        sends_ref[p] = jnp.concatenate([sides[p % 2], *pieces, bias_part], 0)


def close_kernel(terms_ref, back_ref, out_ref):
    sums = [terms_ref[s].astype(F32) for s in range(2)]
    for p in range(2, terms_ref.shape[0]):
        sums[p % 2] += terms_ref[p].astype(F32)
    out_ref[...] = (back_ref[...].astype(F32) + unpacked(sums[0], sums[1])).astype(BF)


def layer(features, edge_rows, edge_cols, weight, bias, upstream, train_mask):
    piece_rows, width = features.shape
    hidden = weight.shape[1]
    slots = edge_rows.shape[-1]
    panel_rows = upstream.shape[0]
    half = piece_rows // 2
    n_blk, n_rep = lax.axis_size("blk"), lax.axis_size("rep")
    panel, place = lax.axis_index("blk"), lax.axis_index("rep")
    planes = [
        [(2 * j + core) * n_rep + 2 * z + s for j in range(n_blk // 2) for s in range(2)]
        for core in range(2)
        for z in range(n_rep // 2)
    ]
    own_rows = edge_rows.reshape(-1, slots)

    left, right = features[:half], features[half:]
    sides = [
        jnp.concatenate([left[:, c : c + HALF], right[:, c : c + HALF]], 1) for c in (0, HALF)
    ]
    sides = jnp.broadcast_to(jnp.stack(sides), (n_blk // 2, 2, half, width)).reshape(-1, half, width)
    table = exchange(sides, ("blk", "rep"), planes)

    other_table = swapped(table, "blk", n_blk, 1)

    edges = jnp.bitwise_or(edge_rows[0], jnp.left_shift(edge_cols[0], 16))
    others = swapped(edges, "rep", n_rep, 1)
    second = jnp.bitwise_and(place, 1) == 1
    both = jnp.stack([jnp.where(second, others, edges), jnp.where(second, edges, others)], 1)
    both = both.reshape(-1, 2, *both.shape[1:]).swapaxes(0, 1).reshape(-1, slots)
    rows = jnp.bitwise_and(both, 0xFFFF)
    cols = jnp.right_shift(both, 16)
    row_list = rows.reshape(-1)

    counts = pl.pallas_call(
        count_kernel,
        in_specs=[VMEM],
        out_specs=VMEM,
        out_shape=jax.ShapeDtypeStruct((panel_rows // LANES, LANES), F32),
        cost_estimate=cost(2),
        name="count",
    )(own_rows)
    chunks = [pltpu.SMEM((CHUNK,), jnp.int32)] * 2 + [pltpu.SemaphoreType.DMA((2,))]

    places = jnp.stack([place, panel]).astype(jnp.int32)
    whole_panel = pltpu.VMEM((panel_rows, width), F32)
    values = [pltpu.VMEM((slots, width), F32)] * 2
    partial = pl.pallas_call(
        functools.partial(gather_sum_kernel, False),
        in_specs=[SMEM, ANY, VMEM, VMEM],
        out_specs=VMEM,
        out_shape=jax.ShapeDtypeStruct((panel_rows, width), F32),
        scratch_shapes=chunks + values + [whole_panel] * TOTALS,
        cost_estimate=cost(10),
        name="gather_own",
    )(places, row_list, cols, table)
    sends = pl.pallas_call(
        functools.partial(gather_sum_kernel, True),
        in_specs=[SMEM, ANY, VMEM, VMEM, VMEM, ANY],
        out_specs=VMEM,
        out_shape=jax.ShapeDtypeStruct((n_rep, half + 8, width), BF),
        scratch_shapes=chunks
        + values
        + [whole_panel, pltpu.SemaphoreType.DMA]
        + [whole_panel] * TOTALS,
        cost_estimate=cost(10),
        name="gather_rest",
    )(places, row_list, cols, other_table, counts, partial)
    parts = exchange(sends, "rep")

    share = width // n_rep
    spans = hidden // LANES
    extra = share * spans + 8
    activations, back, sends = pl.pallas_call(
        dense_kernel,
        grid_spec=pltpu.PrefetchScalarGridSpec(
            num_scalar_prefetch=1,
            grid=(1,),
            in_specs=[
                pl.BlockSpec(parts.shape, lambda i, s: (0, 0, 0)),
                pl.BlockSpec(features.shape, lambda i, s: (0, 0)),
                pl.BlockSpec((piece_rows, hidden), lambda i, s: (s[0], 0)),
                pl.BlockSpec((None, piece_rows // LANES, LANES), lambda i, s: (s[0], 0, 0)),
                pl.BlockSpec(weight.shape, lambda i, s: (0, 0)),
                pl.BlockSpec((1, hidden), lambda i, s: (0, 0)),
            ],
            out_specs=[
                pl.BlockSpec((piece_rows, hidden), lambda i, s: (0, 0)),
                pl.BlockSpec((piece_rows, width), lambda i, s: (0, 0)),
                pl.BlockSpec((n_rep, half + extra, width), lambda i, s: (0, 0, 0)),
            ],
        ),
        out_shape=[
            jax.ShapeDtypeStruct((piece_rows, hidden), BF),
            jax.ShapeDtypeStruct((piece_rows, width), BF),
            jax.ShapeDtypeStruct((n_rep, half + extra, width), BF),
        ],
        cost_estimate=cost(3),
        name="dense",
    )(
        places,
        parts,
        features,
        upstream,
        train_mask.reshape(n_rep, piece_rows // LANES, LANES),
        weight,
        bias.reshape(1, hidden),
    )

    panel_back = exchange(sends, "rep")

    mine = jnp.sum(panel_back[:, half:].astype(F32), axis=0)
    arrived = exchange(jnp.broadcast_to(mine, (n_blk, *mine.shape)), "blk")

    def spread(own):
        return pl.pallas_call(
            functools.partial(spread_kernel, own),
            in_specs=[SMEM, ANY, VMEM, VMEM],
            out_specs=VMEM,
            out_shape=jax.ShapeDtypeStruct((n_blk, half, width), BF),
            scratch_shapes=chunks + [whole_panel] + values,
            cost_estimate=cost(9),
            name="spread_own" if own else "spread_rest",
        )(places, row_list, cols, panel_back)

    rest = spread(False)
    rest = swapped(rest, "blk", n_blk, 1)
    terms = spread(True)
    terms, rest, arrived = lax.optimization_barrier((terms, rest, arrived))
    terms = (terms.astype(F32) + rest.astype(F32)).astype(BF)
    received = exchange(terms, ("blk", "rep"), planes)
    mine = jnp.sum(arrived, axis=0)
    grad_bias = mine[share * spans : share * spans + spans].reshape(hidden)
    shares = mine[: share * spans]
    for bits in (4, 1):
        shares = jnp.stack(
            [shares] + [swapped(shares, "rep", n_rep, bits * d) for d in range(1, 4)]
        )
    low, high = jnp.bitwise_and(place, 3), jnp.right_shift(place, 2)
    for axis, code in ((0, low), (1, high)):
        parts_of = lambda order: jnp.stack([lax.index_in_dim(shares, i, axis, False) for i in order], axis)
        shares = jnp.where(jnp.bitwise_and(code, 1) == 1, parts_of((1, 0, 3, 2)), shares)
        shares = jnp.where(jnp.bitwise_and(code, 2) == 2, parts_of((2, 3, 0, 1)), shares)
    shares = shares.swapaxes(0, 1).reshape(n_rep, spans, share, LANES)
    grad_weight = shares.swapaxes(1, 2).reshape(width, hidden)

    grad_features = pl.pallas_call(
        close_kernel,
        in_specs=[VMEM, VMEM],
        out_specs=VMEM,
        out_shape=jax.ShapeDtypeStruct((piece_rows, width), BF),
        cost_estimate=cost(1),
        name="close",
    )(received, back)
    return (activations, grad_features, grad_weight, grad_bias)


def solution(mesh):
    return jax.shard_map(
        layer,
        mesh=mesh,
        in_specs=(
            P(("blk", "rep"), None),
            P("blk", None, "rep", None),
            P("blk", None, "rep", None),
            P(),
            P(),
            P("blk", None),
            P("blk"),
        ),
        out_specs=(P(("blk", "rep"), None), P(("blk", "rep"), None), P(), P()),
        check_vma=False,
    )
```

```python
import functools

import jax
import jax.numpy as jnp
from jax import lax
from jax.experimental import pallas as pl
from jax.experimental.pallas import tpu as pltpu
from jax.sharding import PartitionSpec as P


CB = 128
LANES = 128
HALF = 64
BF = jnp.bfloat16
F32 = jnp.float32
TN = (((0,), (0,)), ((), ()))
NT = (((1,), (1,)), ((), ()))
TOTALS = 8
CHUNK = 1024

VMEM = pl.BlockSpec(memory_space=pltpu.VMEM)
ANY = pl.BlockSpec(memory_space=pl.ANY)
SMEM = pl.BlockSpec(memory_space=pltpu.SMEM)


def cost(us):
    return pl.CostEstimate(flops=0, transcendentals=0, bytes_accessed=int(us * 3.0e6))


def exchange(parts, axis, groups=None):
    return lax.all_to_all(
        parts, axis, split_axis=0, concat_axis=0, tiled=True, axis_index_groups=groups
    )


def swapped(value, axis, count, bits):
    return lax.ppermute(value, axis, [(i, i ^ bits) for i in range(count)])


def one_hot(index, count):
    hits = lax.broadcasted_iota(jnp.int32, (count, index.shape[-1]), 0) == index
    return hits.astype(F32).astype(BF)


def turned(value):
    return pltpu.roll(value, HALF, 1)


def left_lanes(rows):
    return lax.broadcasted_iota(jnp.int32, (rows, LANES), 1) < HALF


def unpacked(first, second):
    left = left_lanes(first.shape[0])
    top = jnp.where(left, first, turned(second))
    bottom = jnp.where(left, turned(first), second)
    return jnp.concatenate([top, bottom], 0)


def packed(rows):
    half = rows.shape[0] // 2
    left = left_lanes(half)
    top, bottom = rows[:half], rows[half:]
    return jnp.where(left, top, turned(bottom)), jnp.where(left, turned(top), bottom)


def count_kernel(rows_ref, out_ref):
    rows = rows_ref[...]
    total = jnp.zeros(out_ref.shape, F32)
    for k in range(rows.shape[0]):
        index = rows[k : k + 1, :]
        high = one_hot(jnp.right_shift(index, 7), out_ref.shape[0])
        low = one_hot(jnp.bitwise_and(index, LANES - 1), LANES)
        total += lax.dot_general(high, low, NT, preferred_element_type=F32)
    out_ref[...] = total


def gather_sum_kernel(closing, place_ref, rows_ref, cols_ref, table_ref, *refs):
    if closing:
        counts_ref, before_ref, out_ref, list0, list1, sems, values0, values1, held_ref, sem = refs[:10]
        totals = refs[10:]
        pltpu.make_async_copy(before_ref, held_ref, sem).start()
    else:
        out_ref, list0, list1, sems, values0, values1 = refs[:6]
        totals = refs[6:]
    lists, values = (list0, list1), (values0, values1)
    slots = cols_ref.shape[1]
    blocks = cols_ref.shape[0] // 2
    held = CHUNK // slots
    steps = blocks // held // 2
    core = jnp.bitwise_and(place_ref[1], 1)
    base = (1 - core if closing else core) * blocks

    def fetch(step, side):
        start = pl.multiple_of(base * slots + step * CHUNK, CHUNK)
        return pltpu.make_async_copy(rows_ref.at[pl.ds(start, CHUNK)], lists[side], sems.at[side])

    keep = left_lanes(CB).astype(F32).astype(BF)
    keeps = (keep, 1.0 - keep)

    def pick(k, side):
        hits = one_hot(cols_ref[pl.ds(base + k, 1), :], CB)
        block = table_ref[k >> 1] * keeps[side]
        values[side][...] = lax.dot_general(hits, block, TN, preferred_element_type=F32)

    for side in range(2):
        fetch(side, side).start()
    for total in totals:
        total[...] = jnp.zeros_like(total)
    pick(0, 0)

    @pl.loop(0, steps)
    def _(i):
        for side in range(2):
            fetch(2 * i + side, side).wait()
            for s in range(held):
                pick(jnp.minimum((2 * i + side) * held + s + 1, blocks - 1), (s + 1) % 2)
                for u in range(0, slots, TOTALS):
                    rows = [lists[side][s * slots + u + j] for j in range(TOTALS)]
                    olds = [totals[j][pl.ds(rows[j], 1), :] for j in range(TOTALS)]
                    for j in range(TOTALS):
                        new = olds[j] + values[s % 2][u + j : u + j + 1, :]
                        totals[j][pl.ds(rows[j], 1), :] = new

            @pl.when(i < steps - 1)
            def _():
                fetch(2 * i + side + 2, side).start()

    piece_rows = 2 * CB
    left = left_lanes(CB)
    if closing:
        pltpu.make_async_copy(before_ref, held_ref, sem).wait()

    @pl.loop(0, totals[0].shape[0] // piece_rows)
    def _(p):
        span = pl.ds(p * piece_rows, piece_rows)
        part = totals[0][span, :]
        for total in totals[1:]:
            part += total[span, :]
        if not closing:
            out_ref[span, :] = part
            return
        part += held_ref[span, :]
        part += turned(part)
        out_ref[p, :CB, :] = jnp.where(left, part[:CB], part[CB:]).astype(BF)
        groups = piece_rows // LANES
        count = counts_ref[pl.ds(p * groups, groups), :]
        high = jnp.floor(count * (1.0 / 128.0))
        low = count - high * 128.0
        rest = jnp.zeros((8 - 2 * groups, LANES), F32)
        out_ref[p, CB:, :] = jnp.concatenate([high, low, rest], 0).astype(BF)


def spread_kernel(
    own, place_ref, rows_ref, cols_ref, table_ref, out_ref, list0, list1, sems, wide_ref, picked0, picked1
):
    lists, picked = (list0, list1), (picked0, picked1)
    pieces, half = table_ref.shape[0], CB
    slots = cols_ref.shape[1]
    blocks = cols_ref.shape[0] // 2
    held = CHUNK // slots
    steps = blocks // held // 2
    core = jnp.bitwise_and(place_ref[1], 1)
    base = (core if own else 1 - core) * blocks

    def fetch(step, side):
        start = pl.multiple_of(base * slots + step * CHUNK, CHUNK)
        return pltpu.make_async_copy(rows_ref.at[pl.ds(start, CHUNK)], lists[side], sems.at[side])

    for side in range(2):
        fetch(side, side).start()
    for p in range(pieces):
        block = table_ref[p, :half, :].astype(F32)
        wide_ref[p * 2 * half : (p + 1) * 2 * half, :] = unpacked(block, block)
    left = left_lanes(CB)

    @pl.loop(0, steps)
    def _(i):
        for side in range(2):
            fetch(2 * i + side, side).wait()
            terms = [None, None]
            for s in range(held):
                k = (2 * i + side) * held + s
                for u in range(slots):
                    row = wide_ref[pl.ds(lists[side][s * slots + u], 1), :]
                    picked[s % 2][u : u + 1, :] = row
                hits = one_hot(cols_ref[pl.ds(base + k, 1), :], CB)
                terms[s % 2] = jnp.dot(hits, picked[s % 2][...].astype(BF), preferred_element_type=F32)
                if s % 2 == 1:
                    both = jnp.where(left, terms[0], terms[1]).astype(BF)
                    out_ref[k >> 1] = both

            @pl.when(i < steps - 1)
            def _():
                fetch(2 * i + side + 2, side).start()


def as_column(row):
    size = row.shape[1]
    diagonal = lax.broadcasted_iota(jnp.int32, (size, size), 0) == lax.broadcasted_iota(
        jnp.int32, (size, size), 1
    )
    return jnp.sum(jnp.where(diagonal, row, 0.0), axis=1, keepdims=True)


def dense_kernel(
    place_ref, parts_ref, feats_ref, upstream_ref, mask_ref, weight_ref, bias_ref,
    act_ref, back_ref, sends_ref, wsends_ref, wpart_ref,
):
    piece_rows, width = feats_ref.shape
    half = piece_rows // 2
    sums = [parts_ref[s].astype(F32) for s in range(2)]
    for p in range(2, parts_ref.shape[0]):
        sums[p % 2] += parts_ref[p].astype(F32)
    gathered = unpacked(sums[0][:half], sums[1][:half])
    groups = piece_rows // LANES
    numbers = sums[0][half:] + sums[1][half:]
    counts = numbers[:groups] * 128.0 + numbers[groups : 2 * groups]
    degree = 1.0 + jnp.concatenate([as_column(counts[g : g + 1]) for g in range(groups)], 0)
    mask = jnp.concatenate([as_column(mask_ref[g : g + 1].astype(F32)) for g in range(groups)], 0)
    mixed = ((feats_ref[...].astype(F32) + gathered) / degree).astype(BF)
    weight = weight_ref[...]
    pre = jnp.dot(mixed, weight, preferred_element_type=F32) + bias_ref[...]
    gate = 1.0 / (1.0 + jnp.exp(-pre))
    act_ref[...] = (pre * gate).astype(BF)
    slope = gate * (1.0 + pre * (1.0 - gate))
    grad = (upstream_ref[...].astype(F32) * mask * slope).astype(BF)
    back = lax.dot_general(grad, weight, NT, preferred_element_type=F32) / degree
    back = back.astype(BF)
    back_ref[...] = back
    sides = [side.astype(BF) for side in packed(back.astype(F32))]
    for p in range(sends_ref.shape[0]):
        sends_ref[p] = sides[p % 2]
    wpart_ref[...] = lax.dot_general(mixed, grad, TN, preferred_element_type=F32)
    bias_part = jnp.sum(grad.astype(F32), axis=0, keepdims=True)
    spans = range(0, bias_part.shape[1], LANES)
    rest = jnp.zeros((8 - len(spans), LANES), F32)
    bias_part = jnp.concatenate([bias_part[:, c : c + LANES] for c in spans] + [rest], 0)
    count = wsends_ref.shape[0]
    share = width // count
    for d in range(count):
        chip = jnp.bitwise_xor(jnp.right_shift(place_ref[1], 1), d)
        rows = wpart_ref[pl.ds(pl.multiple_of(chip * share, share), share), :]
        wsends_ref[d] = jnp.concatenate([rows[:, c : c + LANES] for c in spans] + [bias_part], 0)


def join_kernel(place_ref, own_ref, rest_ref, shares_ref, out_ref):
    rows = own_ref.shape[1]
    share = (out_ref.shape[1] - rows) // 2
    start = pl.multiple_of(jnp.bitwise_and(place_ref[0], 1) * share, share)
    shares = shares_ref[pl.ds(start, share), :]
    high = shares.astype(BF)
    both = jnp.concatenate([high, (shares - high.astype(F32)).astype(BF)], 0)
    for p in range(out_ref.shape[0]):
        out_ref[p, :rows, :] = (own_ref[p].astype(F32) + rest_ref[p].astype(F32)).astype(BF)
        out_ref[p, rows:, :] = both


def close_kernel(terms_ref, back_ref, out_ref, wgrad_ref):
    rows = back_ref.shape[0] // 2
    sums = [terms_ref[s, :rows].astype(F32) for s in range(2)]
    for p in range(2, terms_ref.shape[0]):
        sums[p % 2] += terms_ref[p, :rows].astype(F32)
    out_ref[...] = (back_ref[...].astype(F32) + unpacked(sums[0], sums[1])).astype(BF)
    share = (terms_ref.shape[1] - rows) // 2
    for p in range(terms_ref.shape[0]):
        both = terms_ref[p, rows : rows + share].astype(F32) + terms_ref[p, rows + share :].astype(F32)
        j, c = p // 2, p % 2
        wgrad_ref[j * share : (j + 1) * share, c * LANES : (c + 1) * LANES] = both


def layer(features, edge_rows, edge_cols, weight, bias, upstream, train_mask):
    piece_rows, width = features.shape
    hidden = weight.shape[1]
    slots = edge_rows.shape[-1]
    panel_rows = upstream.shape[0]
    half = piece_rows // 2
    n_blk, n_rep = lax.axis_size("blk"), lax.axis_size("rep")
    panel, place = lax.axis_index("blk"), lax.axis_index("rep")
    planes = [
        [(2 * j + core) * n_rep + 2 * z + s for j in range(n_blk // 2) for s in range(2)]
        for core in range(2)
        for z in range(n_rep // 2)
    ]
    own_rows = edge_rows.reshape(-1, slots)

    left, right = features[:half], features[half:]
    sides = [
        jnp.concatenate([left[:, c : c + HALF], right[:, c : c + HALF]], 1) for c in (0, HALF)
    ]
    sides = jnp.broadcast_to(jnp.stack(sides), (n_blk // 2, 2, half, width)).reshape(-1, half, width)
    table = exchange(sides, ("blk", "rep"), planes)

    other_table = swapped(table, "blk", n_blk, 1)

    places = jnp.stack([place, panel]).astype(jnp.int32)
    edges = jnp.bitwise_or(edge_rows[0], jnp.left_shift(edge_cols[0], 16))
    others = swapped(edges, "rep", n_rep, 1)
    second = jnp.bitwise_and(place, 1) == 1
    both = jnp.stack([jnp.where(second, others, edges), jnp.where(second, edges, others)], 1)
    both = both.reshape(-1, 2, *both.shape[1:]).swapaxes(0, 1).reshape(-1, slots)
    rows = jnp.bitwise_and(both, 0xFFFF)
    cols = jnp.right_shift(both, 16)
    row_list = rows.reshape(-1)

    counts = pl.pallas_call(
        count_kernel,
        in_specs=[VMEM],
        out_specs=VMEM,
        out_shape=jax.ShapeDtypeStruct((panel_rows // LANES, LANES), F32),
        cost_estimate=cost(2),
        compiler_params=pltpu.CompilerParams(vmem_limit_bytes=8 << 20),
    name="count",
    )(own_rows)
    chunks = [pltpu.SMEM((CHUNK,), jnp.int32)] * 2 + [pltpu.SemaphoreType.DMA((2,))]

    whole_panel = pltpu.VMEM((panel_rows, width), F32)
    values = [pltpu.VMEM((slots, width), F32)] * 2
    partial = pl.pallas_call(
        functools.partial(gather_sum_kernel, False),
        in_specs=[SMEM, ANY, VMEM, VMEM],
        out_specs=VMEM,
        out_shape=jax.ShapeDtypeStruct((panel_rows, width), F32),
        scratch_shapes=chunks + values + [whole_panel] * TOTALS,
        cost_estimate=cost(10),
        compiler_params=pltpu.CompilerParams(vmem_limit_bytes=26 << 20),
        name="gather_own",
    )(places, row_list, cols, table)
    sends = pl.pallas_call(
        functools.partial(gather_sum_kernel, True),
        in_specs=[SMEM, ANY, VMEM, VMEM, VMEM, ANY],
        out_specs=VMEM,
        out_shape=jax.ShapeDtypeStruct((n_rep, half + 8, width), BF),
        scratch_shapes=chunks
        + values
        + [whole_panel, pltpu.SemaphoreType.DMA]
        + [whole_panel] * TOTALS,
        cost_estimate=cost(10),
        compiler_params=pltpu.CompilerParams(vmem_limit_bytes=28 << 20),
        name="gather_rest",
    )(places, row_list, cols, other_table, counts, partial)
    parts = exchange(sends, "rep")

    share = width // (n_blk // 2)
    spans = hidden // LANES
    w_rows = share * spans + 8
    activations, back, sends, wsends = pl.pallas_call(
        dense_kernel,
        grid_spec=pltpu.PrefetchScalarGridSpec(
            num_scalar_prefetch=1,
            grid=(1,),
            in_specs=[
                pl.BlockSpec(parts.shape, lambda i, s: (0, 0, 0)),
                pl.BlockSpec(features.shape, lambda i, s: (0, 0)),
                pl.BlockSpec((piece_rows, hidden), lambda i, s: (s[0], 0)),
                pl.BlockSpec((None, piece_rows // LANES, LANES), lambda i, s: (s[0], 0, 0)),
                pl.BlockSpec(weight.shape, lambda i, s: (0, 0)),
                pl.BlockSpec((1, hidden), lambda i, s: (0, 0)),
            ],
            out_specs=[
                pl.BlockSpec((piece_rows, hidden), lambda i, s: (0, 0)),
                pl.BlockSpec((piece_rows, width), lambda i, s: (0, 0)),
                pl.BlockSpec((n_rep, half, width), lambda i, s: (0, 0, 0)),
                pl.BlockSpec((n_blk // 2, w_rows, LANES), lambda i, s: (0, 0, 0)),
            ],
            scratch_shapes=[pltpu.VMEM((width, hidden), F32)],
        ),
        out_shape=[
            jax.ShapeDtypeStruct((piece_rows, hidden), BF),
            jax.ShapeDtypeStruct((piece_rows, width), BF),
            jax.ShapeDtypeStruct((n_rep, half, width), BF),
            jax.ShapeDtypeStruct((n_blk // 2, w_rows, LANES), F32),
        ],
        cost_estimate=cost(3),
        compiler_params=pltpu.CompilerParams(vmem_limit_bytes=12 << 20),
        name="dense",
    )(
        places,
        parts,
        features,
        upstream,
        train_mask.reshape(n_rep, piece_rows // LANES, LANES),
        weight,
        bias.reshape(1, hidden),
    )

    panel_back = exchange(sends, "rep")

    mine = wsends.reshape(-1, 2, w_rows, LANES)
    near, far = mine[:, 0], mine[:, 1]
    others = [swapped(v, "blk", n_blk, d) for v, d in ((near, 1), (far, 2), (far, 3))]
    near = near + others[0] + others[1] + others[2]
    others = [swapped(near[d], "blk", n_blk, 4 * d) for d in range(1, 4)]
    mine = near[0] + others[0] + others[1] + others[2]
    others = [swapped(mine, "rep", n_rep, d) for d in (4, 8, 12)]

    def spread(own):
        return pl.pallas_call(
            functools.partial(spread_kernel, own),
            in_specs=[SMEM, ANY, VMEM, VMEM],
            out_specs=VMEM,
            out_shape=jax.ShapeDtypeStruct((n_blk, half, width), BF),
            scratch_shapes=chunks + [whole_panel] + values,
            cost_estimate=cost(9),
            compiler_params=pltpu.CompilerParams(vmem_limit_bytes=10 << 20),
            name="spread_own" if own else "spread_rest",
        )(places, row_list, cols, panel_back)

    rest = spread(False)
    arrived = swapped(rest, "blk", n_blk, 1)
    mine = mine + others[0] + others[1] + others[2]
    others = [swapped(mine, "rep", n_rep, d) for d in (1, 2, 3)]
    terms = spread(True)
    mine = mine + others[0] + others[1] + others[2]
    grad_bias = mine[share * spans : share * spans + spans].reshape(hidden)
    joined = pl.pallas_call(
        join_kernel,
        in_specs=[SMEM, VMEM, VMEM, VMEM],
        out_specs=VMEM,
        out_shape=jax.ShapeDtypeStruct((n_blk, half + 2 * share, width), BF),
        cost_estimate=cost(1),
        compiler_params=pltpu.CompilerParams(vmem_limit_bytes=8 << 20),
        name="join",
    )(places, terms, arrived, mine)
    received = exchange(joined, ("blk", "rep"), planes)
    grad_features, grad_weight = pl.pallas_call(
        close_kernel,
        in_specs=[VMEM, VMEM],
        out_specs=[VMEM, VMEM],
        out_shape=[
            jax.ShapeDtypeStruct((piece_rows, width), BF),
            jax.ShapeDtypeStruct((width, hidden), F32),
        ],
        cost_estimate=cost(1),
        compiler_params=pltpu.CompilerParams(vmem_limit_bytes=8 << 20),
        name="close",
    )(received, back)
    return (activations, grad_features, grad_weight, grad_bias)


def solution(mesh):
    return jax.shard_map(
        layer,
        mesh=mesh,
        in_specs=(
            P(("blk", "rep"), None),
            P("blk", None, "rep", None),
            P("blk", None, "rep", None),
            P(),
            P(),
            P("blk", None),
            P("blk"),
        ),
        out_specs=(P(("blk", "rep"), None), P(("blk", "rep"), None), P(), P()),
        check_vma=False,
    )
```

```python
import functools

import jax
import jax.numpy as jnp
from jax import lax
from jax.experimental import pallas as pl
from jax.experimental.pallas import tpu as pltpu
from jax.sharding import PartitionSpec as P


CB = 128
LANES = 128
HALF = 64
BF = jnp.bfloat16
F32 = jnp.float32
TN = (((0,), (0,)), ((), ()))
NT = (((1,), (1,)), ((), ()))
TOTALS = 8
CHUNK = 2048

VMEM = pl.BlockSpec(memory_space=pltpu.VMEM)
ANY = pl.BlockSpec(memory_space=pl.ANY)
SMEM = pl.BlockSpec(memory_space=pltpu.SMEM)


def cost(us):
    return pl.CostEstimate(flops=0, transcendentals=0, bytes_accessed=int(us * 3.0e6))


def exchange(parts, axis, groups=None):
    return lax.all_to_all(
        parts, axis, split_axis=0, concat_axis=0, tiled=True, axis_index_groups=groups
    )


def swapped(value, axis, count, bits):
    return lax.ppermute(value, axis, [(i, i ^ bits) for i in range(count)])


def one_hot(index, count):
    hits = lax.broadcasted_iota(jnp.int32, (count, index.shape[-1]), 0) == index
    return hits.astype(F32).astype(BF)


def turned(value):
    return pltpu.roll(value, HALF, 1)


def left_lanes(rows):
    return lax.broadcasted_iota(jnp.int32, (rows, LANES), 1) < HALF


def unpacked(first, second):
    left = left_lanes(first.shape[0])
    top = jnp.where(left, first, turned(second))
    bottom = jnp.where(left, turned(first), second)
    return jnp.concatenate([top, bottom], 0)


def packed(rows):
    half = rows.shape[0] // 2
    left = left_lanes(half)
    top, bottom = rows[:half], rows[half:]
    return jnp.where(left, top, turned(bottom)), jnp.where(left, turned(top), bottom)


def count_kernel(rows_ref, out_ref):
    rows = rows_ref[...]
    total = jnp.zeros(out_ref.shape, F32)
    for k in range(rows.shape[0]):
        index = rows[k : k + 1, :]
        high = one_hot(jnp.right_shift(index, 7), out_ref.shape[0])
        low = one_hot(jnp.bitwise_and(index, LANES - 1), LANES)
        total += lax.dot_general(high, low, NT, preferred_element_type=F32)
    out_ref[...] = total


def gather_sum_kernel(closing, place_ref, rows_ref, cols_ref, table_ref, *refs):
    if closing:
        counts_ref, refs = refs[0], refs[1 + TOTALS :]
        out_ref, refs = refs[0], refs[1:]
    totals, refs = refs[:TOTALS], refs[TOTALS:]
    list0, list1, sems, values0, values1 = refs
    lists, values = (list0, list1), (values0, values1)
    slots = cols_ref.shape[1]
    blocks = cols_ref.shape[0] // 2
    held = CHUNK // slots
    steps = blocks // held // 2
    core = jnp.bitwise_and(place_ref[1], 1)
    base = (1 - core if closing else core) * blocks

    def fetch(step, side):
        start = pl.multiple_of(base * slots + step * CHUNK, CHUNK)
        return pltpu.make_async_copy(rows_ref.at[pl.ds(start, CHUNK)], lists[side], sems.at[side])

    keep = left_lanes(CB).astype(F32).astype(BF)
    keeps = (keep, 1.0 - keep)

    def pick(k, side):
        hits = one_hot(cols_ref[pl.ds(base + k, 1), :], CB)
        block = table_ref[k >> 1] * keeps[side]
        values[side][...] = lax.dot_general(hits, block, TN, preferred_element_type=F32)

    for side in range(2):
        fetch(side, side).start()
    if not closing:
        for total in totals:
            total[...] = jnp.zeros_like(total)
    pick(0, 0)

    @pl.loop(0, steps)
    def _(i):
        for side in range(2):
            fetch(2 * i + side, side).wait()
            for s in range(held):
                pick(jnp.minimum((2 * i + side) * held + s + 1, blocks - 1), (s + 1) % 2)
                for u in range(0, slots, TOTALS):
                    rows = [lists[side][s * slots + u + j] for j in range(TOTALS)]
                    olds = [totals[j][pl.ds(rows[j], 1), :] for j in range(TOTALS)]
                    for j in range(TOTALS):
                        new = olds[j] + values[s % 2][u + j : u + j + 1, :]
                        totals[j][pl.ds(rows[j], 1), :] = new

            @pl.when(i < steps - 1)
            def _():
                fetch(2 * i + side + 2, side).start()

    if not closing:
        return
    piece_rows = 2 * CB
    left = left_lanes(CB)

    @pl.loop(0, totals[0].shape[0] // piece_rows)
    def _(p):
        span = pl.ds(p * piece_rows, piece_rows)
        part = totals[0][span, :]
        for total in totals[1:]:
            part += total[span, :]
        part += turned(part)
        out_ref[p, :CB, :] = jnp.where(left, part[:CB], part[CB:]).astype(BF)
        groups = piece_rows // LANES
        count = counts_ref[pl.ds(p * groups, groups), :]
        high = jnp.floor(count * (1.0 / 128.0))
        low = count - high * 128.0
        rest = jnp.zeros((8 - 2 * groups, LANES), F32)
        out_ref[p, CB:, :] = jnp.concatenate([high, low, rest], 0).astype(BF)


def spread_kernel(
    own, place_ref, rows_ref, cols_ref, table_ref, out_ref, list0, list1, sems, wide_ref, picked0, picked1
):
    lists, picked = (list0, list1), (picked0, picked1)
    pieces, half = table_ref.shape[0], CB
    slots = cols_ref.shape[1]
    blocks = cols_ref.shape[0] // 2
    held = CHUNK // slots
    steps = blocks // held // 2
    core = jnp.bitwise_and(place_ref[1], 1)
    base = (core if own else 1 - core) * blocks

    def fetch(step, side):
        start = pl.multiple_of(base * slots + step * CHUNK, CHUNK)
        return pltpu.make_async_copy(rows_ref.at[pl.ds(start, CHUNK)], lists[side], sems.at[side])

    for side in range(2):
        fetch(side, side).start()
    for p in range(pieces):
        block = table_ref[p, :half, :].astype(F32)
        wide_ref[p * 2 * half : (p + 1) * 2 * half, :] = unpacked(block, block)
    left = left_lanes(CB)

    @pl.loop(0, steps)
    def _(i):
        for side in range(2):
            fetch(2 * i + side, side).wait()
            terms = [None, None]
            for s in range(held):
                k = (2 * i + side) * held + s
                for u in range(slots):
                    row = wide_ref[pl.ds(lists[side][s * slots + u], 1), :]
                    picked[s % 2][u : u + 1, :] = row
                hits = one_hot(cols_ref[pl.ds(base + k, 1), :], CB)
                terms[s % 2] = jnp.dot(hits, picked[s % 2][...].astype(BF), preferred_element_type=F32)
                if s % 2 == 1:
                    both = jnp.where(left, terms[0], terms[1]).astype(BF)
                    out_ref[k >> 1] = both

            @pl.when(i < steps - 1)
            def _():
                fetch(2 * i + side + 2, side).start()


def as_column(row):
    size = row.shape[1]
    diagonal = lax.broadcasted_iota(jnp.int32, (size, size), 0) == lax.broadcasted_iota(
        jnp.int32, (size, size), 1
    )
    return jnp.sum(jnp.where(diagonal, row, 0.0), axis=1, keepdims=True)


def dense_kernel(
    place_ref, parts_ref, feats_ref, upstream_ref, mask_ref, weight_ref, bias_ref,
    act_ref, back_ref, sends_ref, wsends_ref, wpart_ref,
):
    piece_rows, width = feats_ref.shape
    half = piece_rows // 2
    sums = [parts_ref[s].astype(F32) for s in range(2)]
    for p in range(2, parts_ref.shape[0]):
        sums[p % 2] += parts_ref[p].astype(F32)
    gathered = unpacked(sums[0][:half], sums[1][:half])
    groups = piece_rows // LANES
    numbers = sums[0][half:] + sums[1][half:]
    counts = numbers[:groups] * 128.0 + numbers[groups : 2 * groups]
    degree = 1.0 + jnp.concatenate([as_column(counts[g : g + 1]) for g in range(groups)], 0)
    mask = jnp.concatenate([as_column(mask_ref[g : g + 1].astype(F32)) for g in range(groups)], 0)
    mixed = ((feats_ref[...].astype(F32) + gathered) / degree).astype(BF)
    weight = weight_ref[...]
    pre = jnp.dot(mixed, weight, preferred_element_type=F32) + bias_ref[...]
    gate = 1.0 / (1.0 + jnp.exp(-pre))
    act_ref[...] = (pre * gate).astype(BF)
    slope = gate * (1.0 + pre * (1.0 - gate))
    grad = (upstream_ref[...].astype(F32) * mask * slope).astype(BF)
    back = lax.dot_general(grad, weight, NT, preferred_element_type=F32) / degree
    back = back.astype(BF)
    back_ref[...] = back
    sides = [side.astype(BF) for side in packed(back.astype(F32))]
    for p in range(sends_ref.shape[0]):
        sends_ref[p] = sides[p % 2]
    wpart_ref[...] = lax.dot_general(mixed, grad, TN, preferred_element_type=F32)
    bias_part = jnp.sum(grad.astype(F32), axis=0, keepdims=True)
    spans = range(0, bias_part.shape[1], LANES)
    rest = jnp.zeros((8 - len(spans), LANES), F32)
    bias_part = jnp.concatenate([bias_part[:, c : c + LANES] for c in spans] + [rest], 0)
    count = wsends_ref.shape[0]
    share = width // count
    for d in range(count):
        chip = jnp.bitwise_xor(jnp.right_shift(place_ref[1], 1), d)
        rows = wpart_ref[pl.ds(pl.multiple_of(chip * share, share), share), :]
        wsends_ref[d] = jnp.concatenate([rows[:, c : c + LANES] for c in spans] + [bias_part], 0)


def join_kernel(place_ref, own_ref, rest_ref, shares_ref, out_ref):
    rows = own_ref.shape[1]
    share = (out_ref.shape[1] - rows) // 2
    start = pl.multiple_of(jnp.bitwise_and(place_ref[0], 1) * share, share)
    shares = shares_ref[pl.ds(start, share), :]
    high = shares.astype(BF)
    both = jnp.concatenate([high, (shares - high.astype(F32)).astype(BF)], 0)
    for p in range(out_ref.shape[0]):
        out_ref[p, :rows, :] = (own_ref[p].astype(F32) + rest_ref[p].astype(F32)).astype(BF)
        out_ref[p, rows:, :] = both


def close_kernel(terms_ref, back_ref, out_ref, wgrad_ref):
    rows = back_ref.shape[0] // 2
    sums = [terms_ref[s, :rows].astype(F32) for s in range(2)]
    for p in range(2, terms_ref.shape[0]):
        sums[p % 2] += terms_ref[p, :rows].astype(F32)
    out_ref[...] = (back_ref[...].astype(F32) + unpacked(sums[0], sums[1])).astype(BF)
    share = (terms_ref.shape[1] - rows) // 2
    for p in range(terms_ref.shape[0]):
        both = terms_ref[p, rows : rows + share].astype(F32) + terms_ref[p, rows + share :].astype(F32)
        j, c = p // 2, p % 2
        wgrad_ref[j * share : (j + 1) * share, c * LANES : (c + 1) * LANES] = both


def layer(features, edge_rows, edge_cols, weight, bias, upstream, train_mask):
    piece_rows, width = features.shape
    hidden = weight.shape[1]
    slots = edge_rows.shape[-1]
    panel_rows = upstream.shape[0]
    half = piece_rows // 2
    n_blk, n_rep = lax.axis_size("blk"), lax.axis_size("rep")
    panel, place = lax.axis_index("blk"), lax.axis_index("rep")
    planes = [
        [(2 * j + core) * n_rep + 2 * z + s for j in range(n_blk // 2) for s in range(2)]
        for core in range(2)
        for z in range(n_rep // 2)
    ]
    own_rows = edge_rows.reshape(-1, slots)

    left, right = features[:half], features[half:]
    sides = [
        jnp.concatenate([left[:, c : c + HALF], right[:, c : c + HALF]], 1) for c in (0, HALF)
    ]
    sides = jnp.broadcast_to(jnp.stack(sides), (n_blk // 2, 2, half, width)).reshape(-1, half, width)
    table = exchange(sides, ("blk", "rep"), planes)

    other_table = swapped(table, "blk", n_blk, 1)

    places = jnp.stack([place, panel]).astype(jnp.int32)
    edges = jnp.bitwise_or(edge_rows[0], jnp.left_shift(edge_cols[0], 16))
    others = swapped(edges, "rep", n_rep, 1)
    second = jnp.bitwise_and(place, 1) == 1
    both = jnp.stack([jnp.where(second, others, edges), jnp.where(second, edges, others)], 1)
    both = both.reshape(-1, 2, *both.shape[1:]).swapaxes(0, 1).reshape(-1, slots)
    rows = jnp.bitwise_and(both, 0xFFFF)
    cols = jnp.right_shift(both, 16)
    row_list = rows.reshape(-1)

    counts = pl.pallas_call(
        count_kernel,
        in_specs=[VMEM],
        out_specs=VMEM,
        out_shape=jax.ShapeDtypeStruct((panel_rows // LANES, LANES), F32),
        cost_estimate=cost(2),
        compiler_params=pltpu.CompilerParams(vmem_limit_bytes=8 << 20),
        name="count",
    )(own_rows)
    chunks = [pltpu.SMEM((CHUNK,), jnp.int32)] * 2 + [pltpu.SemaphoreType.DMA((2,))]

    whole_panel = pltpu.VMEM((panel_rows, width), F32)
    values = [pltpu.VMEM((slots, width), F32)] * 2
    total = jax.ShapeDtypeStruct((panel_rows, width), F32)
    totals = pl.pallas_call(
        functools.partial(gather_sum_kernel, False),
        in_specs=[SMEM, ANY, VMEM, VMEM],
        out_specs=[VMEM] * TOTALS,
        out_shape=[total] * TOTALS,
        scratch_shapes=chunks + values,
        cost_estimate=cost(10),
        compiler_params=pltpu.CompilerParams(vmem_limit_bytes=20 << 20),
        name="gather_own",
    )(places, row_list, cols, table)
    sends, *_ = pl.pallas_call(
        functools.partial(gather_sum_kernel, True),
        in_specs=[SMEM, ANY, VMEM, VMEM, VMEM] + [VMEM] * TOTALS,
        out_specs=[VMEM] * (1 + TOTALS),
        out_shape=[jax.ShapeDtypeStruct((n_rep, half + 8, width), BF)] + [total] * TOTALS,
        scratch_shapes=chunks + values,
        input_output_aliases={5 + j: 1 + j for j in range(TOTALS)},
        cost_estimate=cost(10),
        compiler_params=pltpu.CompilerParams(vmem_limit_bytes=20 << 20),
        name="gather_rest",
    )(places, row_list, cols, other_table, counts, *totals)
    parts = exchange(sends, "rep")

    share = width // (n_blk // 2)
    spans = hidden // LANES
    w_rows = share * spans + 8
    activations, back, sends, wsends = pl.pallas_call(
        dense_kernel,
        grid_spec=pltpu.PrefetchScalarGridSpec(
            num_scalar_prefetch=1,
            grid=(1,),
            in_specs=[
                pl.BlockSpec(parts.shape, lambda i, s: (0, 0, 0)),
                pl.BlockSpec(features.shape, lambda i, s: (0, 0)),
                pl.BlockSpec((piece_rows, hidden), lambda i, s: (s[0], 0)),
                pl.BlockSpec((None, piece_rows // LANES, LANES), lambda i, s: (s[0], 0, 0)),
                pl.BlockSpec(weight.shape, lambda i, s: (0, 0)),
                pl.BlockSpec((1, hidden), lambda i, s: (0, 0)),
            ],
            out_specs=[
                pl.BlockSpec((piece_rows, hidden), lambda i, s: (0, 0)),
                pl.BlockSpec((piece_rows, width), lambda i, s: (0, 0)),
                pl.BlockSpec((n_rep, half, width), lambda i, s: (0, 0, 0)),
                pl.BlockSpec((n_blk // 2, w_rows, LANES), lambda i, s: (0, 0, 0)),
            ],
            scratch_shapes=[pltpu.VMEM((width, hidden), F32)],
        ),
        out_shape=[
            jax.ShapeDtypeStruct((piece_rows, hidden), BF),
            jax.ShapeDtypeStruct((piece_rows, width), BF),
            jax.ShapeDtypeStruct((n_rep, half, width), BF),
            jax.ShapeDtypeStruct((n_blk // 2, w_rows, LANES), F32),
        ],
        cost_estimate=cost(3),
        compiler_params=pltpu.CompilerParams(vmem_limit_bytes=12 << 20),
        name="dense",
    )(
        places,
        parts,
        features,
        upstream,
        train_mask.reshape(n_rep, piece_rows // LANES, LANES),
        weight,
        bias.reshape(1, hidden),
    )

    panel_back = exchange(sends, "rep")

    mine = wsends.reshape(-1, 2, w_rows, LANES)
    near, far = mine[:, 0], mine[:, 1]
    others = [swapped(v, "blk", n_blk, d) for v, d in ((near, 1), (far, 2), (far, 3))]
    near = near + others[0] + others[1] + others[2]
    others = [swapped(near[d], "blk", n_blk, 4 * d) for d in range(1, 4)]
    mine = near[0] + others[0] + others[1] + others[2]
    others = [swapped(mine, "rep", n_rep, d) for d in (4, 8, 12)]

    def spread(own):
        return pl.pallas_call(
            functools.partial(spread_kernel, own),
            in_specs=[SMEM, ANY, VMEM, VMEM],
            out_specs=VMEM,
            out_shape=jax.ShapeDtypeStruct((n_blk, half, width), BF),
            scratch_shapes=chunks + [whole_panel] + values,
            cost_estimate=cost(9),
            compiler_params=pltpu.CompilerParams(vmem_limit_bytes=10 << 20),
            name="spread_own" if own else "spread_rest",
        )(places, row_list, cols, panel_back)

    rest = spread(False)
    arrived = swapped(rest, "blk", n_blk, 1)
    mine = mine + others[0] + others[1] + others[2]
    others = [swapped(mine, "rep", n_rep, d) for d in (1, 2, 3)]
    terms = spread(True)
    mine = mine + others[0] + others[1] + others[2]
    grad_bias = mine[share * spans : share * spans + spans].reshape(hidden)
    joined = pl.pallas_call(
        join_kernel,
        in_specs=[SMEM, VMEM, VMEM, VMEM],
        out_specs=VMEM,
        out_shape=jax.ShapeDtypeStruct((n_blk, half + 2 * share, width), BF),
        cost_estimate=cost(1),
        compiler_params=pltpu.CompilerParams(vmem_limit_bytes=8 << 20),
        name="join",
    )(places, terms, arrived, mine)
    received = exchange(joined, ("blk", "rep"), planes)
    grad_features, grad_weight = pl.pallas_call(
        close_kernel,
        in_specs=[VMEM, VMEM],
        out_specs=[VMEM, VMEM],
        out_shape=[
            jax.ShapeDtypeStruct((piece_rows, width), BF),
            jax.ShapeDtypeStruct((width, hidden), F32),
        ],
        cost_estimate=cost(1),
        compiler_params=pltpu.CompilerParams(vmem_limit_bytes=8 << 20),
        name="close",
    )(received, back)
    return (activations, grad_features, grad_weight, grad_bias)


def solution(mesh):
    return jax.shard_map(
        layer,
        mesh=mesh,
        in_specs=(
            P(("blk", "rep"), None),
            P("blk", None, "rep", None),
            P("blk", None, "rep", None),
            P(),
            P(),
            P("blk", None),
            P("blk"),
        ),
        out_specs=(P(("blk", "rep"), None), P(("blk", "rep"), None), P(), P()),
        check_vma=False,
    )
```
